32 devices in a mesh: dp: 8 (over y, x, core), span: 4 (over z).
Axes of the slice: x: 2, y: 2, z: 4, core: 2. Of those that a mesh axis runs over, the one named last changes fastest.
Arguments:
- features: bfloat16 [8, 1024, 1024], P('dp', 'span'), may hold values from -6 to 6
- lengths: int32 [8], P('dp'), may hold values from 256 to 1024, as said below
- labels: int32 [8, 1024], P('dp', 'span'), may hold values from 0 to 4
- w_first: bfloat16 [1024, 1024], replicated, may hold values from -0.1875 to 0.1875
- b_first: float32 [1024], replicated, may hold values from -3 to 3
- w_second: bfloat16 [1024, 256], replicated, may hold values from -0.375 to 0.375
Outputs:
- loss: float32 [], replicated
- grad_first: float32 [1024, 1024], replicated
- grad_bias: float32 [1024], replicated
- grad_second: float32 [1024, 256], replicated
The draws below stay inside these ranges and needn't reach their ends.
Inputs may be any that keep to these rules, and one draw needn't show every extreme that they name: `lengths`: every list has 256 or more real candidates, and some list has exactly 1024.
All inputs are finite; a program needn't handle non-finite values.
Results may differ from the reference program's by a relative error of at most 0.004.
Values may be sent and summed in bfloat16 or wider, within the bound.
A program may use at most 64 MiB of HBM per device.

```python
import math
import jax
import jax.numpy as jnp
from jax import lax

D_IN = 1024
HID = 1024
EMB = 128
CAND_DEV = 256
LIST = 1024
LISTS = 8


def draw_lengths(key, part):
    key_draw, key_chosen = jax.random.split(key)
    sampled = jax.random.randint(key_draw, (LISTS,), CAND_DEV, LIST + 1)
    chosen = jax.random.randint(key_chosen, (), 0, LISTS)
    return jnp.where(jnp.arange(LISTS) == chosen, LIST, sampled).astype(jnp.int32)


def touch_ends(drawn, rng, least, high):
    longest = drawn.shape.index(max(drawn.shape))
    spots = []
    for shift in (0, 1):
        where = [jax.random.randint(jax.random.fold_in(rng, axis), (), 0, length) for axis, length in enumerate(drawn.shape)]
        where[longest] = (where[longest] + shift) % drawn.shape[longest]
        spots.append(tuple(where))
    return drawn.at[spots[0]].set(least).at[spots[1]].set(high)


def block_levels(rng, shape, cuts, smallest, top_value):
    def one(axis_at, parts):
        steps = jax.random.uniform(jax.random.fold_in(jax.random.fold_in(rng, 6), axis_at), (parts,), jnp.float32, smallest / len(cuts), top_value / len(cuts))
        return jnp.repeat(jnp.exp(steps), shape[axis_at] // parts).reshape((-1,) + (1,) * (len(shape) - axis_at - 1))

    loudness = one(*cuts[0])
    for cut in cuts[1:]:
        loudness = loudness * one(*cut)
    return loudness


def bell_draw(stream_key, dims, scale, bound, cuts=(), held_as=jnp.bfloat16):
    factor_of = block_levels(stream_key, dims, cuts, -0.22, 0.18) if cuts else 1.0
    values = jax.random.normal(stream_key, dims, jnp.float32) * scale * factor_of
    return jnp.minimum(jnp.maximum(values, -bound), bound).astype(held_as)


def setup_inputs(seed: int = 0) -> dict:
    key_list = jax.random.split(jax.random.key(seed), 7)
    features = bell_draw(key_list[0], (LISTS, LIST, D_IN), 1.0, 6.0, ((0, 8), (1, 4)))
    lengths = draw_lengths(jax.random.fold_in(key_list[6], 71), 0)
    labels = touch_ends(jax.random.randint(key_list[2], (LISTS, LIST), 0, 5), jax.random.fold_in(key_list[2], 1), 0, 4).astype(jnp.int32)
    w_first = bell_draw(key_list[3], (D_IN, HID), D_IN ** -0.5, 0.1875)
    b_first = bell_draw(key_list[4], (HID,), 0.5, 3.0, (), jnp.float32)
    w_second = bell_draw(key_list[5], (HID, 2 * EMB), (HID // 4) ** -0.5, 0.375)
    return {"features": features, "lengths": lengths, "labels": labels, "w_first": w_first, "b_first": b_first, "w_second": w_second}


gain_values = (0.0, 1.0, 3.0, 7.0, 15.0)
log_two = math.log(2.0)

def level_onehot(labels):
    return (labels[..., None] == jnp.arange(5, dtype=jnp.int32)).astype(jnp.float32)

def ideal_gain(level_counts, list_len):
    levels = jnp.arange(5, dtype=jnp.int32)
    above_mask = (levels[:, None] > levels[None, :]).astype(jnp.float32)
    starts = lax.optimization_barrier(jnp.sum(level_counts[:, None] * above_mask, axis=0))
    finish = starts + level_counts
    places = jnp.arange(1, list_len + 1, dtype=jnp.int32).astype(jnp.float32)
    discount = log_two / jnp.log1p(places)
    inside = (places[None, :] > starts[:, None]) & (places[None, :] <= finish[:, None])
    per_level = lax.optimization_barrier(jnp.sum(jnp.where(inside, discount[None, :], 0.0), axis=1))
    return jnp.maximum(jnp.sum(per_level * jnp.asarray(gain_values, jnp.float32)), 1.0)

def pair_logits(row_emb, key_rows, pair_scale):
    return jnp.einsum('ik,jk->ij', row_emb.astype(jnp.float32), key_rows.astype(jnp.float32), precision=lax.Precision.HIGHEST) * pair_scale

def reference(features, lengths, labels, w_first, b_first, w_second):
    list_count = labels.shape[0]
    list_len = labels.shape[1]
    half_width = w_second.shape[1] // 2
    pair_scale = 1.0 / math.sqrt(half_width)

    def per_list(list_args):
        list_feats, length, list_labels = list_args
        in_list = (jnp.arange(list_len, dtype=jnp.int32) < length).astype(jnp.float32)
        onehot = level_onehot(list_labels) * in_list[:, None]
        gain_row = lax.optimization_barrier(jnp.sum(onehot * jnp.asarray(gain_values, jnp.float32)[None, :], axis=1))
        ideal = ideal_gain(lax.optimization_barrier(jnp.sum(onehot, axis=0)), list_len)
        pre_act = jnp.dot(list_feats, w_first, preferred_element_type=jnp.float32) + b_first[None, :]
        hidden = jnp.maximum(pre_act, 0.0).astype(jnp.bfloat16)
        row_emb = jnp.dot(hidden, w_second, preferred_element_type=jnp.float32).astype(jnp.bfloat16)
        key_rows = jnp.concatenate([row_emb[:, half_width:], -row_emb[:, :half_width]], axis=1)
        emb_blocks = row_emb.reshape(list_len // CAND_DEV, CAND_DEV, 2 * half_width)

        def rank_rows(block_emb):
            logits = pair_logits(block_emb, key_rows, pair_scale)
            return lax.optimization_barrier(jnp.sum(jax.nn.sigmoid(-logits) * in_list[None, :], axis=1))
        soft_rank = 0.5 + lax.map(rank_rows, emb_blocks).reshape(list_len)
        log_rank = jnp.log1p(soft_rank)
        approx_dcg = jnp.sum(gain_row * log_two / log_rank)
        loss_term = (1.0 - approx_dcg / ideal) / list_count
        row_weight = gain_row / (ideal * list_count) * log_two / ((1.0 + soft_rank) * log_rank * log_rank)

        def grad_rows_block(block_args):
            block_emb, block_weight, block_live = block_args
            logits = pair_logits(block_emb, key_rows, pair_scale)
            probab = jax.nn.sigmoid(logits)
            pair_grad = probab * (1.0 - probab) * (block_live[:, None] * row_weight[None, :] - block_weight[:, None] * in_list[None, :])
            return jnp.dot(pair_grad.astype(jnp.bfloat16), key_rows, preferred_element_type=jnp.float32) * pair_scale
        grad_sum = lax.map(grad_rows_block, (emb_blocks, row_weight.reshape(-1, CAND_DEV), in_list.reshape(-1, CAND_DEV)))
        grad_emb = grad_sum.reshape(list_len, 2 * half_width).astype(jnp.bfloat16)
        grad_second = jnp.einsum('ch,ce->he', hidden.astype(jnp.float32), grad_emb.astype(jnp.float32), precision=lax.Precision.HIGHEST)
        back_hidden = jnp.einsum('ce,he->ch', grad_emb.astype(jnp.float32), w_second.astype(jnp.float32), precision=lax.Precision.HIGHEST)
        grad_pre = jnp.where(pre_act > 0.0, back_hidden, 0.0).astype(jnp.bfloat16)
        grad_bias = lax.optimization_barrier(jnp.sum(grad_pre.astype(jnp.float32), axis=0))
        grad_first = jnp.einsum('cd,ch->dh', list_feats.astype(jnp.float32), grad_pre.astype(jnp.float32), precision=lax.Precision.HIGHEST)
        return (grad_first, grad_bias, grad_second, loss_term)
    results = lax.map(per_list, (features, lengths, labels))
    return (jnp.sum(results[3]), lax.optimization_barrier(jnp.sum(results[0], axis=0)), lax.optimization_barrier(jnp.sum(results[1], axis=0)), lax.optimization_barrier(jnp.sum(results[2], axis=0)))
```

```python
import math

import jax
import jax.numpy as jnp
from jax import lax
from jax.experimental import pallas as pl
from jax.experimental.pallas import tpu as pltpu
from jax.sharding import PartitionSpec as P

gain_values = (0.0, 1.0, 3.0, 7.0, 15.0)
log_two = math.log(2.0)


def greet_peers(place, chips, spans):
    core, chip, span = place
    barrier = pltpu.get_barrier_semaphore()
    peers = [{"dp": 2 * chip + 1 - core, "span": span}]
    peers += [{"dp": 2 * lax.rem(chip + k, chips) + core, "span": span} for k in range(1, chips)]
    peers += [{"dp": 2 * chip + core, "span": lax.rem(span + k, spans)} for k in range(1, spans)]
    for peer in peers:
        pl.semaphore_signal(barrier, inc=1, device_id=peer, device_id_type=pl.DeviceIdType.MESH)
    pl.semaphore_wait(barrier, len(peers))


def rows_at(start, size):
    return pl.ds(pl.multiple_of(start, size), size)


def owners_of(rows, chips, spans):
    block = rows // 2 // chips
    return min(spans, block // 16)


class Reducer:
    def __init__(self, place, chips, spans, read, result, small, small_out, scratch):
        self.core, self.chip, self.span = place
        self.chips, self.spans = chips, spans
        self.read, self.result = read, result
        self.small, self.small_out = small, small_out
        (
            self.pair_buf, self.pair_in, self.half_sum, self.half_buf, self.chip_in,
            self.block_sum, self.block_buf, self.span_in,
            self.small_pair, self.small_chip, self.small_span,
            self.pair_s, self.pair_r, self.chip_s, self.chip_r, self.span_s, self.span_r,
            self.small_s, self.small_r,
        ) = scratch
        self.half = self.pair_buf.shape[1]
        self.block = self.half // chips
        self.part = self.span_in.shape[2]
        self.owners = self.block // self.part
        self.copies = {}

    def copy(self, key, src, dst, send, recv, dp=None, span=None):
        peer = {
            "dp": 2 * self.chip + self.core if dp is None else dp,
            "span": self.span if span is None else span,
        }
        made = pltpu.make_async_remote_copy(
            src_ref=src, dst_ref=dst, send_sem=send, recv_sem=recv,
            device_id=peer, device_id_type=pl.DeviceIdType.MESH,
        )
        made.start()
        self.copies.setdefault(key, []).append(made)

    def settle(self, key):
        for made in self.copies.pop(key, []):
            made.wait()

    def partner(self):
        return 2 * self.chip + 1 - self.core

    def other_chip(self, k):
        return 2 * lax.rem(self.chip + k, self.chips) + self.core

    def pair_out(self, p):
        self.pair_buf[p] = self.read(p, rows_at((1 - self.core) * self.half, self.half)).astype(jnp.bfloat16)
        self.copy(("pair", p), self.pair_buf.at[p], self.pair_in.at[p], self.pair_s.at[0, p], self.pair_r.at[0, p], dp=self.partner())

    def chip_out(self, p):
        self.settle(("pair", p))
        own = self.read(p, rows_at(self.core * self.half, self.half))
        total = own + self.pair_in[p].astype(jnp.float32)
        self.half_sum[p] = total
        self.half_buf[p] = total.astype(jnp.bfloat16)
        for k in range(1, self.chips):
            rows = rows_at(lax.rem(self.chip + k, self.chips) * self.block, self.block)
            self.copy(("chip", p), self.half_buf.at[p, rows], self.chip_in.at[p, k - 1], self.chip_s.at[0, p, k - 1], self.chip_r.at[0, p, k - 1], dp=self.other_chip(k))

    def span_out(self, p):
        self.settle(("chip", p))
        total = self.half_sum[p, rows_at(self.chip * self.block, self.block)]
        for k in range(1, self.chips):
            total = total + self.chip_in[p, k - 1].astype(jnp.float32)
        self.block_sum[p] = total
        self.block_buf[p] = total.astype(jnp.bfloat16)
        for k in range(1, self.spans):
            to = lax.rem(self.span + k, self.spans)
            rows = rows_at(lax.rem(to, self.owners) * self.part, self.part)
            self.copy(("span", p), self.block_buf.at[p, rows], self.span_in.at[p, k - 1], self.span_s.at[0, p, k - 1], self.span_r.at[0, p, k - 1], span=to)

    def span_back(self, p):
        self.settle(("span", p))
        mine = lax.rem(self.span, self.owners)
        rows = rows_at(mine * self.part, self.part)
        if self.owners == self.spans:
            total = self.block_sum[p, rows]
        else:
            total = self.block_buf[p, rows].astype(jnp.float32)
        for k in range(1, self.spans):
            total = total + self.span_in[p, k - 1].astype(jnp.float32)
        start = self.core * self.half + self.chip * self.block + mine * self.part
        place = self.result(p, rows_at(start, self.part))
        place[...] = total.astype(jnp.bfloat16)
        for k in range(1, self.owners):
            to = self.span - mine + lax.rem(mine + k, self.owners)
            self.copy(("span_back", p), place, place, self.span_s.at[1, p, k - 1], self.span_r.at[1, p, k - 1], span=to)

    def chip_back(self, p):
        self.settle(("span_back", p))
        place = self.result(p, rows_at(self.core * self.half + self.chip * self.block, self.block))
        for k in range(1, self.chips):
            self.copy(("chip_back", p), place, place, self.chip_s.at[1, p, k - 1], self.chip_r.at[1, p, k - 1], dp=self.other_chip(k))

    def pair_back(self, p):
        self.settle(("chip_back", p))
        place = self.result(p, rows_at(self.core * self.half, self.half))
        self.copy(("pair_back", p), place, place, self.pair_s.at[1, p], self.pair_r.at[1, p], dp=self.partner())

    def small_first(self):
        self.small_pair[self.core] = self.small()
        place = self.small_pair.at[self.core]
        self.copy("small0", place, place, self.small_s.at[0], self.small_r.at[0], dp=self.partner())

    def small_second(self):
        self.settle("small0")
        self.small_chip[self.chip] = self.small_pair[0] + self.small_pair[1]
        place = self.small_chip.at[self.chip]
        for k in range(1, self.chips):
            self.copy("small1", place, place, self.small_s.at[k], self.small_r.at[k], dp=self.other_chip(k))

    def small_third(self):
        self.settle("small1")
        total = self.small_chip[0]
        for k in range(1, self.chips):
            total = total + self.small_chip[k]
        self.small_span[self.span] = total
        place = self.small_span.at[self.span]
        for k in range(1, self.spans):
            at = self.chips + k - 1
            self.copy("small2", place, place, self.small_s.at[at], self.small_r.at[at], span=lax.rem(self.span + k, self.spans))

    def small_last(self):
        self.settle("small2")
        total = self.small_span[0]
        for k in range(1, self.spans):
            total = total + self.small_span[k]
        self.small_out[...] = total


def reducer_scratch(pieces, rows, width, chips, spans, small_shape):
    half = rows // 2
    block = half // chips
    part = block // owners_of(rows, chips, spans)
    vmem, dma = pltpu.VMEM, pltpu.SemaphoreType.DMA
    return [
        vmem((pieces, half, width), jnp.bfloat16),
        vmem((pieces, half, width), jnp.bfloat16),
        vmem((pieces, half, width), jnp.float32),
        vmem((pieces, half, width), jnp.bfloat16),
        vmem((pieces, chips - 1, block, width), jnp.bfloat16),
        vmem((pieces, block, width), jnp.float32),
        vmem((pieces, block, width), jnp.bfloat16),
        vmem((pieces, spans - 1, part, width), jnp.bfloat16),
        vmem((2,) + small_shape, jnp.float32),
        vmem((chips,) + small_shape, jnp.float32),
        vmem((spans,) + small_shape, jnp.float32),
        dma((2, pieces)), dma((2, pieces)),
        dma((2, pieces, chips - 1)), dma((2, pieces, chips - 1)),
        dma((2, pieces, spans - 1)), dma((2, pieces, spans - 1)),
        dma((chips + spans,)), dma((chips + spans,)),
    ]


def finish_reduce(red, pieces):
    red.small_second()
    for p in range(pieces):
        red.span_out(p)
    red.small_third()
    for p in range(pieces):
        red.span_back(p)
    red.small_last()
    for p in range(pieces):
        red.chip_back(p)
    for p in range(pieces):
        red.pair_back(p)
    for p in range(pieces):
        red.settle(("pair_back", p))


def sum_kernel(chips, spans, first, second, small, first_out, second_out, small_out, *scratch):
    dp = lax.axis_index("dp")
    place = (lax.rem(dp, 2), dp // 2, lax.axis_index("span"))
    width = second.shape[1]
    pieces = 1 + first.shape[1] // width

    def read(p, rows):
        return second[rows, :] if p == 0 else first[rows, pl.ds((p - 1) * width, width)]

    def result(p, rows):
        return second_out.at[rows] if p == 0 else first_out.at[rows, pl.ds((p - 1) * width, width)]

    red = Reducer(place, chips, spans, read, result, lambda: small[...], small_out, scratch)
    greet_peers(place, chips, spans)
    for p in range(pieces):
        red.pair_out(p)
    red.small_first()
    for p in range(pieces):
        red.chip_out(p)
    finish_reduce(red, pieces)


def sum_over_devices(first, bias, second, loss):
    chips, spans = lax.axis_size("dp") // 2, lax.axis_size("span")
    rows, width = second.shape
    pieces = 1 + first.shape[1] // width
    small = jnp.concatenate([bias.reshape(-1, 128), jnp.broadcast_to(loss, (8, 128))], axis=0)
    in_vmem = pl.BlockSpec(memory_space=pltpu.VMEM)
    first_sum, second_sum, small_sum = pl.pallas_call(
        lambda *refs: sum_kernel(chips, spans, *refs),
        name="device_sum",
        out_shape=(
            jax.ShapeDtypeStruct(first.shape, jnp.bfloat16),
            jax.ShapeDtypeStruct(second.shape, jnp.bfloat16),
            jax.ShapeDtypeStruct(small.shape, jnp.float32),
        ),
        in_specs=[in_vmem] * 3,
        out_specs=(in_vmem,) * 3,
        scratch_shapes=reducer_scratch(pieces, rows, width, chips, spans, small.shape),
        compiler_params=pltpu.CompilerParams(collective_id=0, has_side_effects=True, vmem_limit_bytes=60 << 20),
    )(first, second, small)
    return (
        first_sum.astype(jnp.float32),
        small_sum[:-8].reshape(bias.shape),
        second_sum.astype(jnp.float32),
        small_sum[-8, 0],
    )


def level_onehot(labels):
    return (labels[..., None] == jnp.arange(5, dtype=jnp.int32)).astype(jnp.float32)


def ideal_gain(level_counts, list_len):
    levels = jnp.arange(5, dtype=jnp.int32)
    above_mask = (levels[:, None] > levels[None, :]).astype(jnp.float32)
    starts = jnp.sum(level_counts[:, None] * above_mask, axis=0)
    finish = starts + level_counts
    places = jnp.arange(1, list_len + 1, dtype=jnp.int32).astype(jnp.float32)
    discount = log_two / jnp.log1p(places)
    inside = (places[None, :] > starts[:, None]) & (places[None, :] <= finish[:, None])
    per_level = jnp.sum(jnp.where(inside, discount[None, :], 0.0), axis=1)
    return jnp.maximum(jnp.sum(per_level * jnp.asarray(gain_values, jnp.float32)), 1.0)


def rank_part(row_emb, block_keys, block_mask, pair_scale):
    logits = (
        jnp.einsum("ik,jk->ij", row_emb, block_keys, preferred_element_type=jnp.float32)
        * pair_scale
    )
    return jnp.sum(jax.nn.sigmoid(-logits) * block_mask.astype(jnp.float32)[None, :], axis=1)


def grad_part(row_emb, row_weight, row_mask, block_keys, key_weight, key_mask, pair_scale):
    logits = (
        jnp.einsum("ik,jk->ij", row_emb, block_keys, preferred_element_type=jnp.float32)
        * pair_scale
    )
    probab = jax.nn.sigmoid(logits)
    pair_grad = (
        probab
        * (1.0 - probab)
        * (row_mask[:, None] * key_weight[None, :] - row_weight[:, None] * key_mask[None, :])
    )
    return (
        jnp.dot(pair_grad.astype(jnp.bfloat16), block_keys, preferred_element_type=jnp.float32)
        * pair_scale
    )


def shards(features, lengths, labels, w_first, b_first, w_second):
    row_feats = features[0]
    row_count = row_feats.shape[0]
    half_width = w_second.shape[1] // 2
    pair_scale = 1.0 / math.sqrt(half_width)
    span_count = lax.axis_size("span")
    list_count = lax.axis_size("dp")
    list_len = row_count * span_count
    row_start = lax.axis_index("span") * row_count
    length = lengths[0]
    in_list = (row_start + jnp.arange(row_count, dtype=jnp.int32) < length).astype(jnp.float32)
    onehot = level_onehot(labels[0]) * in_list[:, None]
    gain_row = jnp.sum(onehot * jnp.asarray(gain_values, jnp.float32)[None, :], axis=1)
    level_counts = lax.psum(jnp.sum(onehot, axis=0), "span")
    ideal = ideal_gain(level_counts, list_len)
    pre_act = jnp.dot(row_feats, w_first, preferred_element_type=jnp.float32) + b_first[None, :]
    hidden = jnp.maximum(pre_act, 0.0).astype(jnp.bfloat16)
    row_emb = jnp.dot(hidden, w_second, preferred_element_type=jnp.float32).astype(jnp.bfloat16)
    key_rows = jnp.concatenate([row_emb[:, half_width:], -row_emb[:, :half_width]], axis=1)
    mask_half = in_list.astype(jnp.bfloat16)
    result = rank_part(
        row_emb,
        lax.all_gather(key_rows, "span", axis=0, tiled=True),
        lax.all_gather(mask_half, "span", axis=0, tiled=True),
        pair_scale,
    )
    rank_sum = result
    soft_rank = 0.5 + rank_sum
    log_rank = jnp.log1p(soft_rank)
    approx_dcg = jnp.sum(gain_row * log_two / log_rank)
    loss_part = (1.0 / span_count - approx_dcg / ideal) / list_count
    row_weight = (
        gain_row / (ideal * list_count) * log_two / ((1.0 + soft_rank) * log_rank * log_rank)
    )
    all_weight, all_live = (
        lax.all_gather(row_weight, "span", axis=0, tiled=True),
        lax.all_gather(in_list, "span", axis=0, tiled=True),
    )
    result = grad_part(
        row_emb,
        row_weight,
        in_list,
        lax.all_gather(key_rows, "span", axis=0, tiled=True),
        all_weight,
        all_live,
        pair_scale,
    )
    grad_emb = result.astype(jnp.bfloat16)
    grad_second = jnp.einsum("ch,ce->he", hidden, grad_emb, preferred_element_type=jnp.float32)
    back_hidden = jnp.einsum("ce,he->ch", grad_emb, w_second, preferred_element_type=jnp.float32)
    grad_pre = jnp.where(pre_act > 0.0, back_hidden, 0.0).astype(jnp.bfloat16)
    grad_bias = jnp.sum(grad_pre.astype(jnp.float32), axis=0)
    grad_first = jnp.einsum("cd,ch->dh", row_feats, grad_pre, preferred_element_type=jnp.float32)
    total_first, total_bias, total_second, loss = sum_over_devices(
        grad_first, grad_bias, grad_second, loss_part
    )
    return (loss, total_first, total_bias, total_second)


def solution(mesh):
    placed = (P("dp", "span", None), P("dp"), P("dp", "span"), P(), P(), P())
    return jax.shard_map(
        shards, mesh=mesh, in_specs=placed, out_specs=(P(), P(), P(), P()), check_vma=False
    )
```

```python
import math

import jax
import jax.numpy as jnp
from jax import lax
from jax.experimental import pallas as pl
from jax.experimental.pallas import tpu as pltpu
from jax.sharding import PartitionSpec as P

gain_values = (0.0, 1.0, 3.0, 7.0, 15.0)
log_two = math.log(2.0)


def greet_peers(place, chips, spans):
    core, chip, span = place
    barrier = pltpu.get_barrier_semaphore()
    peers = [{"dp": 2 * chip + 1 - core, "span": span}]
    peers += [{"dp": 2 * lax.rem(chip + k, chips) + core, "span": span} for k in range(1, chips)]
    peers += [{"dp": 2 * chip + core, "span": lax.rem(span + k, spans)} for k in range(1, spans)]
    for peer in peers:
        pl.semaphore_signal(barrier, inc=1, device_id=peer, device_id_type=pl.DeviceIdType.MESH)
    return lambda: pl.semaphore_wait(barrier, len(peers))


def rows_at(start, size):
    return pl.ds(pl.multiple_of(start, size), size)


def owners_of(rows, chips, spans):
    block = rows // 2 // chips
    return min(spans, block // 16)


class Reducer:
    def __init__(self, place, chips, spans, read, result, small, small_out, scratch):
        self.core, self.chip, self.span = place
        self.chips, self.spans = chips, spans
        self.read, self.result = read, result
        self.small, self.small_out = small, small_out
        (
            self.pair_buf, self.pair_in, self.half_sum, self.half_buf, self.chip_in,
            self.block_sum, self.block_buf, self.span_in,
            self.small_pair, self.small_chip, self.small_span,
            self.pair_s, self.pair_r, self.chip_s, self.chip_r, self.span_s, self.span_r,
            self.small_s, self.small_r,
        ) = scratch
        self.half = self.pair_buf.shape[1]
        self.block = self.half // chips
        self.part = self.span_in.shape[2]
        self.owners = self.block // self.part
        self.copies = {}

    def copy(self, key, src, dst, send, recv, dp=None, span=None):
        peer = {
            "dp": 2 * self.chip + self.core if dp is None else dp,
            "span": self.span if span is None else span,
        }
        made = pltpu.make_async_remote_copy(
            src_ref=src, dst_ref=dst, send_sem=send, recv_sem=recv,
            device_id=peer, device_id_type=pl.DeviceIdType.MESH,
        )
        made.start()
        self.copies.setdefault(key, []).append(made)

    def settle(self, key):
        for made in self.copies.pop(key, []):
            made.wait()

    def partner(self):
        return 2 * self.chip + 1 - self.core

    def other_chip(self, k):
        return 2 * lax.rem(self.chip + k, self.chips) + self.core

    def pair_out(self, p):
        self.pair_buf[p] = self.read(p, rows_at((1 - self.core) * self.half, self.half)).astype(jnp.bfloat16)
        self.copy(("pair", p), self.pair_buf.at[p], self.pair_in.at[p], self.pair_s.at[0, p], self.pair_r.at[0, p], dp=self.partner())

    def chip_out(self, p):
        self.settle(("pair", p))
        own = self.read(p, rows_at(self.core * self.half, self.half))
        total = own + self.pair_in[p].astype(jnp.float32)
        self.half_sum[p] = total
        self.half_buf[p] = total.astype(jnp.bfloat16)
        for k in range(1, self.chips):
            rows = rows_at(lax.rem(self.chip + k, self.chips) * self.block, self.block)
            self.copy(("chip", p), self.half_buf.at[p, rows], self.chip_in.at[p, k - 1], self.chip_s.at[0, p, k - 1], self.chip_r.at[0, p, k - 1], dp=self.other_chip(k))

    def span_out(self, p):
        self.settle(("chip", p))
        total = self.half_sum[p, rows_at(self.chip * self.block, self.block)]
        for k in range(1, self.chips):
            total = total + self.chip_in[p, k - 1].astype(jnp.float32)
        self.block_sum[p] = total
        self.block_buf[p] = total.astype(jnp.bfloat16)
        for k in range(1, self.spans):
            to = lax.rem(self.span + k, self.spans)
            rows = rows_at(lax.rem(to, self.owners) * self.part, self.part)
            self.copy(("span", p), self.block_buf.at[p, rows], self.span_in.at[p, k - 1], self.span_s.at[0, p, k - 1], self.span_r.at[0, p, k - 1], span=to)

    def span_back(self, p):
        self.settle(("span", p))
        mine = lax.rem(self.span, self.owners)
        rows = rows_at(mine * self.part, self.part)
        if self.owners == self.spans:
            total = self.block_sum[p, rows]
        else:
            total = self.block_buf[p, rows].astype(jnp.float32)
        for k in range(1, self.spans):
            total = total + self.span_in[p, k - 1].astype(jnp.float32)
        start = self.core * self.half + self.chip * self.block + mine * self.part
        place = self.result(p, rows_at(start, self.part))
        place[...] = total.astype(jnp.bfloat16)
        for k in range(1, self.owners):
            to = self.span - mine + lax.rem(mine + k, self.owners)
            self.copy(("span_back", p), place, place, self.span_s.at[1, p, k - 1], self.span_r.at[1, p, k - 1], span=to)

    def chip_back(self, p):
        self.settle(("span_back", p))
        place = self.result(p, rows_at(self.core * self.half + self.chip * self.block, self.block))
        for k in range(1, self.chips):
            self.copy(("chip_back", p), place, place, self.chip_s.at[1, p, k - 1], self.chip_r.at[1, p, k - 1], dp=self.other_chip(k))

    def pair_back(self, p):
        self.settle(("chip_back", p))
        place = self.result(p, rows_at(self.core * self.half, self.half))
        self.copy(("pair_back", p), place, place, self.pair_s.at[1, p], self.pair_r.at[1, p], dp=self.partner())

    def small_first(self):
        self.small_pair[self.core] = self.small()
        place = self.small_pair.at[self.core]
        self.copy("small0", place, place, self.small_s.at[0], self.small_r.at[0], dp=self.partner())

    def small_second(self):
        self.settle("small0")
        self.small_chip[self.chip] = self.small_pair[0] + self.small_pair[1]
        place = self.small_chip.at[self.chip]
        for k in range(1, self.chips):
            self.copy("small1", place, place, self.small_s.at[k], self.small_r.at[k], dp=self.other_chip(k))

    def small_third(self):
        self.settle("small1")
        total = self.small_chip[0]
        for k in range(1, self.chips):
            total = total + self.small_chip[k]
        self.small_span[self.span] = total
        place = self.small_span.at[self.span]
        for k in range(1, self.spans):
            at = self.chips + k - 1
            self.copy("small2", place, place, self.small_s.at[at], self.small_r.at[at], span=lax.rem(self.span + k, self.spans))

    def small_last(self):
        self.settle("small2")
        total = self.small_span[0]
        for k in range(1, self.spans):
            total = total + self.small_span[k]
        self.small_out[...] = total


def reducer_scratch(pieces, rows, width, chips, spans, small_shape):
    half = rows // 2
    block = half // chips
    part = block // owners_of(rows, chips, spans)
    vmem, dma = pltpu.VMEM, pltpu.SemaphoreType.DMA
    return [
        vmem((pieces, half, width), jnp.bfloat16),
        vmem((pieces, half, width), jnp.bfloat16),
        vmem((pieces, half, width), jnp.float32),
        vmem((pieces, half, width), jnp.bfloat16),
        vmem((pieces, chips - 1, block, width), jnp.bfloat16),
        vmem((pieces, block, width), jnp.float32),
        vmem((pieces, block, width), jnp.bfloat16),
        vmem((pieces, spans - 1, part, width), jnp.bfloat16),
        vmem((2,) + small_shape, jnp.float32),
        vmem((chips,) + small_shape, jnp.float32),
        vmem((spans,) + small_shape, jnp.float32),
        dma((2, pieces)), dma((2, pieces)),
        dma((2, pieces, chips - 1)), dma((2, pieces, chips - 1)),
        dma((2, pieces, spans - 1)), dma((2, pieces, spans - 1)),
        dma((chips + spans,)), dma((chips + spans,)),
    ]


def finish_reduce(red, pieces):
    red.small_second()
    for p in range(pieces):
        red.span_out(p)
    red.small_third()
    for p in range(pieces):
        red.span_back(p)
    red.small_last()
    for p in range(pieces):
        red.chip_back(p)
    for p in range(pieces):
        red.pair_back(p)
    for p in range(pieces):
        red.settle(("pair_back", p))


def dot(lhs, rhs, dims):
    return lax.dot_general(lhs, rhs, (dims, ((), ())), preferred_element_type=jnp.float32)


def ideal_gain(counts, list_len):
    places = (1 + lax.broadcasted_iota(jnp.int32, (1, list_len), 1)).astype(jnp.float32)
    discount = log_two / jnp.log(1.0 + places)
    total = jnp.zeros((1, 1), jnp.float32)
    start = jnp.zeros((1, 1), jnp.float32)
    for level in reversed(range(len(gain_values))):
        finish = start + counts[level : level + 1, 0:1]
        inside = (places > start) & (places <= finish)
        total = total + gain_values[level] * jnp.sum(jnp.where(inside, discount, 0.0), axis=1, keepdims=True)
        start = finish
    return jnp.maximum(total, 1.0)


def step_kernel(
    chips, spans, lengths, labels, features_hbm, w_first_hbm, b_first, w_second_hbm,
    first_out, second_out, small_out,
    feats, w_first, w_second, feats_t, hidden_t, pre, hidden, emb, keys, slopes, weights, counts, grads, small,
    load_sem, key_s, key_r, weight_s, weight_r, count_s, count_r, *scratch,
):
    dp, span = lax.axis_index("dp"), lax.axis_index("span")
    place = (lax.rem(dp, 2), dp // 2, span)
    rows = feats.shape[0]
    width = w_second.shape[1]
    hid = w_first.shape[1]
    half_width = width // 2
    pair_scale = 1.0 / math.sqrt(half_width)
    pieces = 1 + hid // width
    list_count, list_len = 2 * chips, rows * spans
    loads = [
        pltpu.make_async_copy(src, dst, load_sem.at[n])
        for n, (src, dst) in enumerate(
            ((features_hbm.at[0], feats), (w_first_hbm, w_first), (w_second_hbm, w_second))
        )
    ]
    for load in loads:
        load.start()
    enter = greet_peers(place, chips, spans)

    def to_peers(make_src, dst, send, recv):
        made = []
        for k in range(1, spans):
            copy = pltpu.make_async_remote_copy(
                src_ref=make_src, dst_ref=dst.at[k], send_sem=send.at[k - 1], recv_sem=recv.at[k - 1],
                device_id={"dp": dp, "span": lax.rem(span + k, spans)}, device_id_type=pl.DeviceIdType.MESH,
            )
            copy.start()
            made.append(copy)
        return made

    length = lengths[0]
    slots = lax.broadcasted_iota(jnp.int32, (1, rows), 1)

    def live_row(k):
        owner = lax.rem(span - k + spans, spans)
        return (owner * rows + slots < length).astype(jnp.float32)

    own_live = live_row(0)
    live_col = (span * rows + lax.broadcasted_iota(jnp.int32, (rows, 1), 0) < length).astype(jnp.float32)
    eye = lax.broadcasted_iota(jnp.int32, (rows, rows), 0) == lax.broadcasted_iota(jnp.int32, (rows, rows), 1)
    label_row = labels[...].astype(jnp.float32)
    label_col = jnp.sum(jnp.where(eye, label_row, 0.0), axis=1, keepdims=True)
    gain = jnp.zeros((rows, 1), jnp.float32)
    for level, value in enumerate(gain_values):
        gain = gain + jnp.where(label_col == level, value, 0.0)
    gain = gain * live_col
    levels = lax.broadcasted_iota(jnp.int32, (8, rows), 0).astype(jnp.float32)
    level_counts = jnp.sum(jnp.where(levels == label_row, own_live, 0.0), axis=1, keepdims=True)
    counts[0] = jnp.broadcast_to(level_counts, counts.shape[1:])

    loads[0].wait()
    loads[1].wait()
    for p in range(pieces - 1):
        cols = pl.ds(p * width, width)
        pre_act = dot(feats[...], w_first[:, cols], ((1,), (0,))) + b_first[:, cols]
        pre[:, cols] = pre_act
        hidden[:, cols] = jnp.maximum(pre_act, 0.0).astype(jnp.bfloat16)
    loads[2].wait()
    row_emb = dot(hidden[...], w_second[...], ((1,), (0,))).astype(jnp.bfloat16)
    emb[...] = row_emb
    keys[0] = jnp.concatenate([row_emb[:, half_width:], -row_emb[:, :half_width]], axis=1)
    enter()
    key_copies = to_peers(keys.at[0], keys, key_s, key_r)
    count_copies = to_peers(counts.at[0], counts, count_s, count_r)
    feats_t[...] = feats[...].T
    hidden_t[...] = hidden[...].T

    rank = jnp.full((rows, 1), 0.5, jnp.float32)
    for k in range(spans):
        if k:
            key_copies[k - 1].wait()
        logits = dot(emb[...], keys[k], ((1,), (1,))) * pair_scale
        below = jax.nn.sigmoid(-logits)
        slopes[k] = below * (1.0 - below)
        rank = rank + jnp.sum(below * live_row(k), axis=1, keepdims=True)
    for copy in count_copies:
        copy.wait()
    all_counts = counts[0]
    for k in range(1, spans):
        all_counts = all_counts + counts[k]
    ideal = ideal_gain(all_counts, list_len)
    log_rank = jnp.log(1.0 + rank)
    weight = gain / (ideal * list_count) * log_two / ((1.0 + rank) * log_rank * log_rank)
    weights[0] = jnp.broadcast_to(jnp.sum(jnp.where(eye, weight, 0.0), axis=0, keepdims=True), weights.shape[1:])
    weight_copies = to_peers(weights.at[0], weights, weight_s, weight_r)
    dcg = jnp.sum(gain * log_two / log_rank, axis=0, keepdims=True)
    loss_part = (1.0 / spans - dcg / ideal) / list_count
    small[:, pl.ds(hid, 128)] = jnp.broadcast_to(loss_part, (1, 128))

    total = jnp.zeros((rows, width), jnp.float32)
    for k in range(spans):
        if k:
            weight_copies[k - 1].wait()
        pair_grad = slopes[k] * (live_col * weights[k, 0:1, :] - weight * live_row(k))
        total = total + dot(pair_grad.astype(jnp.bfloat16), keys[k], ((1,), (0,)))
    grad_emb = (total * pair_scale).astype(jnp.bfloat16)

    def read(p, at):
        return grads[p, at, :]

    def result(p, at):
        return second_out.at[at] if p == 0 else first_out.at[at, pl.ds((p - 1) * width, width)]

    red = Reducer(place, chips, spans, read, result, lambda: small[...], small_out, scratch)
    grads[0] = dot(hidden_t[...], grad_emb, ((1,), (0,)))
    red.pair_out(0)
    for p in range(1, pieces):
        cols = pl.ds((p - 1) * width, width)
        back = dot(grad_emb, w_second[cols, :], ((1,), (1,)))
        grad_pre = jnp.where(pre[:, cols] > 0.0, back, 0.0).astype(jnp.bfloat16)
        small[:, cols] = jnp.sum(grad_pre.astype(jnp.float32), axis=0, keepdims=True)
        grads[p] = dot(feats_t[...], grad_pre, ((1,), (0,)))
        red.pair_out(p)
        red.chip_out(p - 1)
    red.small_first()
    red.chip_out(pieces - 1)
    finish_reduce(red, pieces)


def shards(features, lengths, labels, w_first, b_first, w_second):
    chips, spans = lax.axis_size("dp") // 2, lax.axis_size("span")
    rows, depth = features.shape[1:]
    hid, width = w_second.shape
    pieces = 1 + hid // width
    small_shape = (1, hid + 128)
    vmem, dma = pltpu.VMEM, pltpu.SemaphoreType.DMA
    in_vmem = pl.BlockSpec(memory_space=pltpu.VMEM)
    in_place = pl.BlockSpec(memory_space=pl.ANY)
    first_sum, second_sum, small_sum = pl.pallas_call(
        lambda *refs: step_kernel(chips, spans, *refs),
        name="rank_step",
        out_shape=(
            jax.ShapeDtypeStruct((depth, hid), jnp.bfloat16),
            jax.ShapeDtypeStruct((hid, width), jnp.bfloat16),
            jax.ShapeDtypeStruct(small_shape, jnp.float32),
        ),
        in_specs=[pl.BlockSpec(memory_space=pltpu.SMEM), in_vmem, in_place, in_place, in_vmem, in_place],
        out_specs=(in_vmem,) * 3,
        scratch_shapes=[
            vmem((rows, depth), jnp.bfloat16),
            vmem((depth, hid), jnp.bfloat16),
            vmem((hid, width), jnp.bfloat16),
            vmem((depth, rows), jnp.bfloat16),
            vmem((hid, rows), jnp.bfloat16),
            vmem((rows, hid), jnp.float32),
            vmem((rows, hid), jnp.bfloat16),
            vmem((rows, width), jnp.bfloat16),
            vmem((spans, rows, width), jnp.bfloat16),
            vmem((spans, rows, rows), jnp.float32),
            vmem((spans, 8, rows), jnp.float32),
            vmem((spans, 8, 128), jnp.float32),
            vmem((pieces, hid, width), jnp.float32),
            vmem(small_shape, jnp.float32),
            dma((3,)),
            dma((spans - 1,)), dma((spans - 1,)), dma((spans - 1,)),
            dma((spans - 1,)), dma((spans - 1,)), dma((spans - 1,)),
        ]
        + reducer_scratch(pieces, hid, width, chips, spans, small_shape),
        compiler_params=pltpu.CompilerParams(collective_id=0, has_side_effects=True, vmem_limit_bytes=60 << 20),
    )(lengths, labels, features, w_first, b_first.reshape(1, -1), w_second)
    return (
        small_sum[0, hid],
        first_sum.astype(jnp.float32),
        small_sum[0, :hid],
        second_sum.astype(jnp.float32),
    )


def solution(mesh):
    placed = (P("dp", "span", None), P("dp"), P("dp", "span"), P(), P(), P())
    return jax.shard_map(
        shards, mesh=mesh, in_specs=placed, out_specs=(P(), P(), P(), P()), check_vma=False
    )
```

```python
import math

import jax
import jax.numpy as jnp
from jax import lax
from jax.experimental import pallas as pl
from jax.experimental.pallas import tpu as pltpu
from jax.sharding import PartitionSpec as P

gain_values = (0.0, 1.0, 3.0, 7.0, 15.0)
log_two = math.log(2.0)


def greet_peers(place, chips, spans):
    core, chip, span = place
    barrier = pltpu.get_barrier_semaphore()
    peers = [{"dp": 2 * chip + 1 - core, "span": span}]
    peers += [{"dp": 2 * lax.rem(chip + k, chips) + core, "span": span} for k in range(1, chips)]
    peers += [{"dp": 2 * chip + core, "span": lax.rem(span + k, spans)} for k in range(1, spans)]
    for peer in peers:
        pl.semaphore_signal(barrier, inc=1, device_id=peer, device_id_type=pl.DeviceIdType.MESH)
    return lambda: pl.semaphore_wait(barrier, len(peers))


def rows_at(start, size):
    return pl.ds(pl.multiple_of(start, size), size)


def owners_of(rows, chips, spans):
    block = rows // 2 // chips
    return min(spans, block // 16)


class Reducer:
    def __init__(self, place, chips, spans, read, result, small, small_out, scratch):
        self.core, self.chip, self.span = place
        self.chips, self.spans = chips, spans
        self.read, self.result = read, result
        self.small, self.small_out = small, small_out
        (
            self.pair_buf, self.pair_in, self.half_sum, self.half_buf, self.chip_in,
            self.block_sum, self.block_buf, self.span_in,
            self.small_pair, self.small_chip, self.small_span,
            self.pair_s, self.pair_r, self.chip_s, self.chip_r, self.span_s, self.span_r,
            self.small_s, self.small_r,
        ) = scratch
        self.half = self.pair_buf.shape[1]
        self.block = self.half // chips
        self.part = self.span_in.shape[2]
        self.owners = self.block // self.part
        self.copies = {}

    def copy(self, key, src, dst, send, recv, dp=None, span=None):
        peer = {
            "dp": 2 * self.chip + self.core if dp is None else dp,
            "span": self.span if span is None else span,
        }
        made = pltpu.make_async_remote_copy(
            src_ref=src, dst_ref=dst, send_sem=send, recv_sem=recv,
            device_id=peer, device_id_type=pl.DeviceIdType.MESH,
        )
        made.start()
        self.copies.setdefault(key, []).append(made)

    def settle(self, key):
        for made in self.copies.pop(key, []):
            made.wait()

    def partner(self):
        return 2 * self.chip + 1 - self.core

    def other_chip(self, k):
        return 2 * lax.rem(self.chip + k, self.chips) + self.core

    def pair_out(self, p):
        self.pair_buf[p] = self.read(p, rows_at((1 - self.core) * self.half, self.half)).astype(jnp.bfloat16)
        self.copy(("pair", p), self.pair_buf.at[p], self.pair_in.at[p], self.pair_s.at[0, p], self.pair_r.at[0, p], dp=self.partner())

    def chip_out(self, p):
        self.settle(("pair", p))
        own = self.read(p, rows_at(self.core * self.half, self.half))
        total = own + self.pair_in[p].astype(jnp.float32)
        self.half_sum[p] = total
        self.half_buf[p] = total.astype(jnp.bfloat16)
        for k in range(1, self.chips):
            rows = rows_at(lax.rem(self.chip + k, self.chips) * self.block, self.block)
            self.copy(("chip", p), self.half_buf.at[p, rows], self.chip_in.at[p, k - 1], self.chip_s.at[0, p, k - 1], self.chip_r.at[0, p, k - 1], dp=self.other_chip(k))

    def span_out(self, p):
        self.settle(("chip", p))
        total = self.half_sum[p, rows_at(self.chip * self.block, self.block)]
        for k in range(1, self.chips):
            total = total + self.chip_in[p, k - 1].astype(jnp.float32)
        self.block_sum[p] = total
        self.block_buf[p] = total.astype(jnp.bfloat16)
        for k in range(1, self.spans):
            to = lax.rem(self.span + k, self.spans)
            rows = rows_at(lax.rem(to, self.owners) * self.part, self.part)
            self.copy(("span", p), self.block_buf.at[p, rows], self.span_in.at[p, k - 1], self.span_s.at[0, p, k - 1], self.span_r.at[0, p, k - 1], span=to)

    def span_back(self, p):
        self.settle(("span", p))
        mine = lax.rem(self.span, self.owners)
        rows = rows_at(mine * self.part, self.part)
        if self.owners == self.spans:
            total = self.block_sum[p, rows]
        else:
            total = self.block_buf[p, rows].astype(jnp.float32)
        for k in range(1, self.spans):
            total = total + self.span_in[p, k - 1].astype(jnp.float32)
        start = self.core * self.half + self.chip * self.block + mine * self.part
        place = self.result(p, rows_at(start, self.part))
        place[...] = total.astype(jnp.bfloat16)
        for k in range(1, self.owners):
            to = self.span - mine + lax.rem(mine + k, self.owners)
            self.copy(("span_back", p), place, place, self.span_s.at[1, p, k - 1], self.span_r.at[1, p, k - 1], span=to)

    def chip_back(self, p):
        self.settle(("span_back", p))
        place = self.result(p, rows_at(self.core * self.half + self.chip * self.block, self.block))
        for k in range(1, self.chips):
            self.copy(("chip_back", p), place, place, self.chip_s.at[1, p, k - 1], self.chip_r.at[1, p, k - 1], dp=self.other_chip(k))

    def pair_back(self, p):
        self.settle(("chip_back", p))
        place = self.result(p, rows_at(self.core * self.half, self.half))
        self.copy(("pair_back", p), place, place, self.pair_s.at[1, p], self.pair_r.at[1, p], dp=self.partner())

    def small_first(self):
        self.small_pair[self.core] = self.small()
        place = self.small_pair.at[self.core]
        self.copy("small0", place, place, self.small_s.at[0], self.small_r.at[0], dp=self.partner())

    def small_second(self):
        self.settle("small0")
        self.small_chip[self.chip] = self.small_pair[0] + self.small_pair[1]
        place = self.small_chip.at[self.chip]
        for k in range(1, self.chips):
            self.copy("small1", place, place, self.small_s.at[k], self.small_r.at[k], dp=self.other_chip(k))

    def small_third(self):
        self.settle("small1")
        total = self.small_chip[0]
        for k in range(1, self.chips):
            total = total + self.small_chip[k]
        self.small_span[self.span] = total
        place = self.small_span.at[self.span]
        for k in range(1, self.spans):
            at = self.chips + k - 1
            self.copy("small2", place, place, self.small_s.at[at], self.small_r.at[at], span=lax.rem(self.span + k, self.spans))

    def small_last(self):
        self.settle("small2")
        total = self.small_span[0]
        for k in range(1, self.spans):
            total = total + self.small_span[k]
        self.small_out[...] = total


def reducer_scratch(pieces, rows, width, chips, spans, small_shape):
    half = rows // 2
    block = half // chips
    part = block // owners_of(rows, chips, spans)
    vmem, dma = pltpu.VMEM, pltpu.SemaphoreType.DMA
    return [
        vmem((pieces, half, width), jnp.bfloat16),
        vmem((pieces, half, width), jnp.bfloat16),
        vmem((pieces, half, width), jnp.float32),
        vmem((pieces, half, width), jnp.bfloat16),
        vmem((pieces, chips - 1, block, width), jnp.bfloat16),
        vmem((pieces, block, width), jnp.float32),
        vmem((pieces, block, width), jnp.bfloat16),
        vmem((pieces, spans - 1, part, width), jnp.bfloat16),
        vmem((2,) + small_shape, jnp.float32),
        vmem((chips,) + small_shape, jnp.float32),
        vmem((spans,) + small_shape, jnp.float32),
        dma((2, pieces)), dma((2, pieces)),
        dma((2, pieces, chips - 1)), dma((2, pieces, chips - 1)),
        dma((2, pieces, spans - 1)), dma((2, pieces, spans - 1)),
        dma((chips + spans,)), dma((chips + spans,)),
    ]


def finish_reduce(red, pieces):
    stages = (red.span_out, red.span_back, red.chip_back, red.pair_back, lambda p: red.settle(("pair_back", p)))
    smalls = {0: red.small_second, 1: red.small_third, 3: red.small_last}
    for turn in range(pieces + len(stages) - 1):
        for lag, stage in enumerate(stages):
            if 0 <= turn - lag < pieces:
                stage(turn - lag)
        if turn in smalls:
            smalls[turn]()


def write_kernel(first, second, small, first_out, second_out, bias_out, loss_out, first_buf, second_buf, sem):
    parts = first_buf.shape[0]
    rows = first_buf.shape[1]
    copies = [pltpu.make_async_copy(second_buf, second_out, sem.at[parts])]
    second_buf[...] = second[...].astype(jnp.float32)
    copies[0].start()
    for n in range(parts):
        at = pl.ds(n * rows, rows)
        first_buf[n] = first[at, :].astype(jnp.float32)
        copies.append(pltpu.make_async_copy(first_buf.at[n], first_out.at[at], sem.at[n]))
        copies[-1].start()
    hid = bias_out.shape[1]
    bias_out[...] = small[:, pl.ds(0, hid)]
    loss_out[...] = small[:, pl.ds(hid, 1)]
    for copy in copies:
        copy.wait()


def dot(lhs, rhs, dims):
    return lax.dot_general(lhs, rhs, (dims, ((), ())), preferred_element_type=jnp.float32)


def ideal_gain(counts, list_len):
    places = (1 + lax.broadcasted_iota(jnp.int32, (1, list_len), 1)).astype(jnp.float32)
    discount = log_two / jnp.log(1.0 + places)
    total = jnp.zeros((1, 1), jnp.float32)
    start = jnp.zeros((1, 1), jnp.float32)
    for level in reversed(range(len(gain_values))):
        finish = start + counts[level : level + 1, 0:1]
        inside = (places > start) & (places <= finish)
        total = total + gain_values[level] * jnp.sum(jnp.where(inside, discount, 0.0), axis=1, keepdims=True)
        start = finish
    return jnp.maximum(total, 1.0)


def step_kernel(
    chips, spans, lengths, labels, features_hbm, w_first_hbm, b_first, w_second_hbm,
    first_out, second_out, small_out,
    feats, w_first, w_second, feats_t, hidden_t, pre, hidden, emb, keys, slopes, weights, counts, grads, small,
    load_sem, key_s, key_r, weight_s, weight_r, count_s, count_r, *scratch,
):
    dp, span = lax.axis_index("dp"), lax.axis_index("span")
    place = (lax.rem(dp, 2), dp // 2, span)
    rows = feats.shape[0]
    width = w_second.shape[1]
    hid = w_first.shape[1]
    half_width = width // 2
    pair_scale = 1.0 / math.sqrt(half_width)
    pieces = 1 + hid // width
    list_count, list_len = 2 * chips, rows * spans
    loads = [
        pltpu.make_async_copy(src, dst, load_sem.at[n])
        for n, (src, dst) in enumerate(
            ((features_hbm.at[0], feats), (w_first_hbm, w_first), (w_second_hbm, w_second))
        )
    ]
    for load in loads:
        load.start()
    enter = greet_peers(place, chips, spans)

    def to_peers(make_src, dst, send, recv):
        made = []
        for k in range(1, spans):
            copy = pltpu.make_async_remote_copy(
                src_ref=make_src, dst_ref=dst.at[k], send_sem=send.at[k - 1], recv_sem=recv.at[k - 1],
                device_id={"dp": dp, "span": lax.rem(span + k, spans)}, device_id_type=pl.DeviceIdType.MESH,
            )
            copy.start()
            made.append(copy)
        return made

    length = lengths[0]
    slots = lax.broadcasted_iota(jnp.int32, (1, rows), 1)

    def live_row(k):
        owner = lax.rem(span - k + spans, spans)
        return (owner * rows + slots < length).astype(jnp.float32)

    own_live = live_row(0)
    live_col = (span * rows + lax.broadcasted_iota(jnp.int32, (rows, 1), 0) < length).astype(jnp.float32)
    eye = lax.broadcasted_iota(jnp.int32, (rows, rows), 0) == lax.broadcasted_iota(jnp.int32, (rows, rows), 1)
    label_row = labels[...].astype(jnp.float32)
    label_col = jnp.sum(jnp.where(eye, label_row, 0.0), axis=1, keepdims=True)
    gain = jnp.zeros((rows, 1), jnp.float32)
    for level, value in enumerate(gain_values):
        gain = gain + jnp.where(label_col == level, value, 0.0)
    gain = gain * live_col
    levels = lax.broadcasted_iota(jnp.int32, (8, rows), 0).astype(jnp.float32)
    level_counts = jnp.sum(jnp.where(levels == label_row, own_live, 0.0), axis=1, keepdims=True)
    counts[0] = jnp.broadcast_to(level_counts, counts.shape[1:])

    loads[0].wait()
    loads[1].wait()
    for p in range(pieces - 1):
        cols = pl.ds(p * width, width)
        pre_act = dot(feats[...], w_first[:, cols], ((1,), (0,))) + b_first[:, cols]
        pre[:, cols] = pre_act
        hidden[:, cols] = jnp.maximum(pre_act, 0.0).astype(jnp.bfloat16)
    loads[2].wait()
    row_emb = dot(hidden[...], w_second[...], ((1,), (0,))).astype(jnp.bfloat16)
    emb[...] = row_emb
    keys[0] = jnp.concatenate([row_emb[:, half_width:], -row_emb[:, :half_width]], axis=1)
    enter()
    key_copies = to_peers(keys.at[0], keys, key_s, key_r)
    count_copies = to_peers(counts.at[0], counts, count_s, count_r)
    feats_t[...] = feats[...].T
    hidden_t[...] = hidden[...].T

    rank = jnp.full((rows, 1), 0.5, jnp.float32)
    for k in range(spans):
        if k:
            key_copies[k - 1].wait()
        logits = dot(emb[...], keys[k], ((1,), (1,))) * pair_scale
        below = jax.nn.sigmoid(-logits)
        slopes[k] = below * (1.0 - below)
        rank = rank + jnp.sum(below * live_row(k), axis=1, keepdims=True)
    for copy in count_copies:
        copy.wait()
    all_counts = counts[0]
    for k in range(1, spans):
        all_counts = all_counts + counts[k]
    ideal = ideal_gain(all_counts, list_len)
    log_rank = jnp.log(1.0 + rank)
    weight = gain / (ideal * list_count) * log_two / ((1.0 + rank) * log_rank * log_rank)
    weights[0] = jnp.broadcast_to(jnp.sum(jnp.where(eye, weight, 0.0), axis=0, keepdims=True), weights.shape[1:])
    weight_copies = to_peers(weights.at[0], weights, weight_s, weight_r)
    dcg = jnp.sum(gain * log_two / log_rank, axis=0, keepdims=True)
    loss_part = (1.0 / spans - dcg / ideal) / list_count
    small[:, pl.ds(hid, 128)] = jnp.broadcast_to(loss_part, (1, 128))

    total = jnp.zeros((rows, width), jnp.float32)
    for k in range(spans):
        if k:
            weight_copies[k - 1].wait()
        pair_grad = slopes[k] * (live_col * weights[k, 0:1, :] - weight * live_row(k))
        total = total + dot(pair_grad.astype(jnp.bfloat16), keys[k], ((1,), (0,)))
    grad_emb = (total * pair_scale).astype(jnp.bfloat16)

    def read(p, at):
        return grads[p, at, :]

    def result(p, at):
        return second_out.at[at] if p == 0 else first_out.at[at, pl.ds((p - 1) * width, width)]

    red = Reducer(place, chips, spans, read, result, lambda: small[...], small_out, scratch)
    grads[0] = dot(hidden_t[...], grad_emb, ((1,), (0,)))
    red.pair_out(0)
    for p in range(1, pieces):
        cols = pl.ds((p - 1) * width, width)
        back = dot(grad_emb, w_second[cols, :], ((1,), (1,)))
        grad_pre = jnp.where(pre[:, cols] > 0.0, back, 0.0).astype(jnp.bfloat16)
        small[:, cols] = jnp.sum(grad_pre.astype(jnp.float32), axis=0, keepdims=True)
        grads[p] = dot(feats_t[...], grad_pre, ((1,), (0,)))
        red.pair_out(p)
        red.chip_out(p - 1)
    red.small_first()
    red.chip_out(pieces - 1)
    finish_reduce(red, pieces)


def shards(features, lengths, labels, w_first, b_first, w_second):
    chips, spans = lax.axis_size("dp") // 2, lax.axis_size("span")
    rows, depth = features.shape[1:]
    hid, width = w_second.shape
    pieces = 1 + hid // width
    small_shape = (1, hid + 128)
    vmem, dma = pltpu.VMEM, pltpu.SemaphoreType.DMA
    in_vmem = pl.BlockSpec(memory_space=pltpu.VMEM)
    in_place = pl.BlockSpec(memory_space=pl.ANY)
    first_sum, second_sum, small_sum = pl.pallas_call(
        lambda *refs: step_kernel(chips, spans, *refs),
        name="rank_step",
        out_shape=(
            jax.ShapeDtypeStruct((depth, hid), jnp.bfloat16),
            jax.ShapeDtypeStruct((hid, width), jnp.bfloat16),
            jax.ShapeDtypeStruct(small_shape, jnp.float32),
        ),
        in_specs=[pl.BlockSpec(memory_space=pltpu.SMEM), in_vmem, in_place, in_place, in_vmem, in_place],
        out_specs=(in_vmem,) * 3,
        scratch_shapes=[
            vmem((rows, depth), jnp.bfloat16),
            vmem((depth, hid), jnp.bfloat16),
            vmem((hid, width), jnp.bfloat16),
            vmem((depth, rows), jnp.bfloat16),
            vmem((hid, rows), jnp.bfloat16),
            vmem((rows, hid), jnp.float32),
            vmem((rows, hid), jnp.bfloat16),
            vmem((rows, width), jnp.bfloat16),
            vmem((spans, rows, width), jnp.bfloat16),
            vmem((spans, rows, rows), jnp.float32),
            vmem((spans, 8, rows), jnp.float32),
            vmem((spans, 8, 128), jnp.float32),
            vmem((pieces, hid, width), jnp.float32),
            vmem(small_shape, jnp.float32),
            dma((3,)),
            dma((spans - 1,)), dma((spans - 1,)), dma((spans - 1,)),
            dma((spans - 1,)), dma((spans - 1,)), dma((spans - 1,)),
        ]
        + reducer_scratch(pieces, hid, width, chips, spans, small_shape),
        compiler_params=pltpu.CompilerParams(collective_id=0, has_side_effects=True, vmem_limit_bytes=60 << 20),
    )(lengths, labels, features, w_first, b_first.reshape(1, -1), w_second)
    parts = 4
    first, second, bias, loss = pl.pallas_call(
        write_kernel,
        name="write_out",
        out_shape=(
            jax.ShapeDtypeStruct((depth, hid), jnp.float32),
            jax.ShapeDtypeStruct((hid, width), jnp.float32),
            jax.ShapeDtypeStruct((1, hid), jnp.float32),
            jax.ShapeDtypeStruct((1, 1), jnp.float32),
        ),
        in_specs=[in_vmem] * 3,
        out_specs=(in_place, in_place, in_vmem, in_vmem),
        scratch_shapes=[
            vmem((parts, depth // parts, hid), jnp.float32),
            vmem((hid, width), jnp.float32),
            dma((parts + 1,)),
        ],
    )(first_sum, second_sum, small_sum)
    return loss[0, 0], first, bias[0], second


def solution(mesh):
    placed = (P("dp", "span", None), P("dp"), P("dp", "span"), P(), P(), P())
    return jax.shard_map(
        shards, mesh=mesh, in_specs=placed, out_specs=(P(), P(), P(), P()), check_vma=False
    )
```

```python
import math

import jax
import jax.numpy as jnp
from jax import lax
from jax.experimental import pallas as pl
from jax.experimental.pallas import tpu as pltpu
from jax.sharding import PartitionSpec as P

gain_values = (0.0, 1.0, 3.0, 7.0, 15.0)
log_two = math.log(2.0)


def greet_peers(place, chips, spans):
    core, chip, span = place
    barrier = pltpu.get_barrier_semaphore()
    peers = [{"dp": 2 * chip + 1 - core, "span": span}]
    peers += [{"dp": 2 * lax.rem(chip + k, chips) + core, "span": span} for k in range(1, chips)]
    peers += [{"dp": 2 * chip + core, "span": lax.rem(span + k, spans)} for k in range(1, spans)]
    for peer in peers:
        pl.semaphore_signal(barrier, inc=1, device_id=peer, device_id_type=pl.DeviceIdType.MESH)
    return lambda: pl.semaphore_wait(barrier, len(peers))


def rows_at(start, size):
    return pl.ds(pl.multiple_of(start, size), size)


def owners_of(rows, chips, spans):
    block = rows // 2 // chips
    return min(spans, block // 16)


class Reducer:
    def __init__(self, place, chips, spans, grads, result, small, small_out, scratch):
        self.core, self.chip, self.span = place
        self.chips, self.spans = chips, spans
        self.grads, self.result = grads, result
        self.small, self.small_out = small, small_out
        (
            self.pair_in, self.half_sum, self.half_buf, self.chip_in,
            self.block_sum, self.block_buf, self.span_in,
            self.small_pair, self.small_chip, self.small_span,
            self.pair_s, self.pair_r, self.chip_s, self.chip_r, self.span_s, self.span_r,
            self.small_s, self.small_r,
        ) = scratch
        self.half = self.pair_in.shape[1]
        self.block = self.half // chips
        self.part = self.span_in.shape[2]
        self.owners = self.block // self.part
        self.copies = {}

    def copy(self, key, src, dst, send, recv, dp=None, span=None):
        peer = {
            "dp": 2 * self.chip + self.core if dp is None else dp,
            "span": self.span if span is None else span,
        }
        made = pltpu.make_async_remote_copy(
            src_ref=src, dst_ref=dst, send_sem=send, recv_sem=recv,
            device_id=peer, device_id_type=pl.DeviceIdType.MESH,
        )
        made.start()
        self.copies.setdefault(key, []).append(made)

    def settle(self, key):
        for made in self.copies.pop(key, []):
            made.wait()

    def partner(self):
        return 2 * self.chip + 1 - self.core

    def other_chip(self, k):
        return 2 * lax.rem(self.chip + k, self.chips) + self.core

    def pair_out(self, p):
        away = self.grads.at[p, rows_at((1 - self.core) * self.half, self.half)]
        self.copy(("pair", p), away, self.pair_in.at[p], self.pair_s.at[0, p], self.pair_r.at[0, p], dp=self.partner())

    def chip_out(self, p):
        self.settle(("pair", p))
        own = self.grads[p, rows_at(self.core * self.half, self.half), :]
        total = own + self.pair_in[p]
        self.half_sum[p] = total
        self.half_buf[p] = total.astype(jnp.bfloat16)
        for k in range(1, self.chips):
            rows = rows_at(lax.rem(self.chip + k, self.chips) * self.block, self.block)
            self.copy(("chip", p), self.half_buf.at[p, rows], self.chip_in.at[p, k - 1], self.chip_s.at[0, p, k - 1], self.chip_r.at[0, p, k - 1], dp=self.other_chip(k))

    def span_out(self, p):
        self.settle(("chip", p))
        total = self.half_sum[p, rows_at(self.chip * self.block, self.block)]
        for k in range(1, self.chips):
            total = total + self.chip_in[p, k - 1].astype(jnp.float32)
        self.block_sum[p] = total
        self.block_buf[p] = total.astype(jnp.bfloat16)
        for k in range(1, self.spans):
            to = lax.rem(self.span + k, self.spans)
            rows = rows_at(lax.rem(to, self.owners) * self.part, self.part)
            self.copy(("span", p), self.block_buf.at[p, rows], self.span_in.at[p, k - 1], self.span_s.at[0, p, k - 1], self.span_r.at[0, p, k - 1], span=to)

    def span_back(self, p):
        self.settle(("span", p))
        mine = lax.rem(self.span, self.owners)
        rows = rows_at(mine * self.part, self.part)
        if self.owners == self.spans:
            total = self.block_sum[p, rows]
        else:
            total = self.block_buf[p, rows].astype(jnp.float32)
        for k in range(1, self.spans):
            total = total + self.span_in[p, k - 1].astype(jnp.float32)
        start = self.core * self.half + self.chip * self.block + mine * self.part
        place = self.result(p, rows_at(start, self.part))
        place[...] = total.astype(jnp.bfloat16)
        for k in range(1, self.owners):
            to = self.span - mine + lax.rem(mine + k, self.owners)
            self.copy(("span_back", p), place, place, self.span_s.at[1, p, k - 1], self.span_r.at[1, p, k - 1], span=to)

    def chip_back(self, p):
        self.settle(("span_back", p))
        place = self.result(p, rows_at(self.core * self.half + self.chip * self.block, self.block))
        for k in range(1, self.chips):
            self.copy(("chip_back", p), place, place, self.chip_s.at[1, p, k - 1], self.chip_r.at[1, p, k - 1], dp=self.other_chip(k))

    def pair_back(self, p):
        self.settle(("chip_back", p))
        place = self.result(p, rows_at(self.core * self.half, self.half))
        self.copy(("pair_back", p), place, place, self.pair_s.at[1, p], self.pair_r.at[1, p], dp=self.partner())

    def small_first(self):
        self.small_pair[self.core] = self.small()
        place = self.small_pair.at[self.core]
        self.copy("small0", place, place, self.small_s.at[0], self.small_r.at[0], dp=self.partner())

    def small_second(self):
        self.settle("small0")
        self.small_chip[self.chip] = self.small_pair[0] + self.small_pair[1]
        place = self.small_chip.at[self.chip]
        for k in range(1, self.chips):
            self.copy("small1", place, place, self.small_s.at[k], self.small_r.at[k], dp=self.other_chip(k))

    def small_third(self):
        self.settle("small1")
        total = self.small_chip[0]
        for k in range(1, self.chips):
            total = total + self.small_chip[k]
        self.small_span[self.span] = total
        place = self.small_span.at[self.span]
        for k in range(1, self.spans):
            at = self.chips + k - 1
            self.copy("small2", place, place, self.small_s.at[at], self.small_r.at[at], span=lax.rem(self.span + k, self.spans))

    def small_last(self):
        self.settle("small2")
        total = self.small_span[0]
        for k in range(1, self.spans):
            total = total + self.small_span[k]
        self.small_out[...] = total


def reducer_scratch(pieces, rows, width, chips, spans, small_shape):
    half = rows // 2
    block = half // chips
    part = block // owners_of(rows, chips, spans)
    vmem, dma = pltpu.VMEM, pltpu.SemaphoreType.DMA
    return [
        vmem((pieces, half, width), jnp.float32),
        vmem((pieces, half, width), jnp.float32),
        vmem((pieces, half, width), jnp.bfloat16),
        vmem((pieces, chips - 1, block, width), jnp.bfloat16),
        vmem((pieces, block, width), jnp.float32),
        vmem((pieces, block, width), jnp.bfloat16),
        vmem((pieces, spans - 1, part, width), jnp.bfloat16),
        vmem((2,) + small_shape, jnp.float32),
        vmem((chips,) + small_shape, jnp.float32),
        vmem((spans,) + small_shape, jnp.float32),
        dma((2, pieces)), dma((2, pieces)),
        dma((2, pieces, chips - 1)), dma((2, pieces, chips - 1)),
        dma((2, pieces, spans - 1)), dma((2, pieces, spans - 1)),
        dma((chips + spans,)), dma((chips + spans,)),
    ]


def finish_reduce(red, pieces):
    stages = (red.span_out, red.span_back, red.chip_back, red.pair_back, lambda p: red.settle(("pair_back", p)))
    order = sorted((p + lag, n, p) for p in range(pieces) for n, lag in enumerate((0, 2.2, 4.3, 6.5, 9.0)))
    smalls = {0: red.small_second, 3: red.small_third, 8: red.small_last}
    for at, (_, n, p) in enumerate(order):
        stages[n](p)
        if at in smalls:
            smalls[at]()


def write_kernel(first, second, small, first_out, second_out, bias_out, loss_out, first_buf, second_buf, sem):
    parts = first_buf.shape[0]
    rows = first_buf.shape[1]
    copies = [pltpu.make_async_copy(second_buf, second_out, sem.at[parts])]
    second_buf[...] = second[...].astype(jnp.float32)
    copies[0].start()
    for n in range(parts):
        at = pl.ds(n * rows, rows)
        first_buf[n] = first[at, :].astype(jnp.float32)
        copies.append(pltpu.make_async_copy(first_buf.at[n], first_out.at[at], sem.at[n]))
        copies[-1].start()
    hid = bias_out.shape[1]
    bias_out[...] = small[:, pl.ds(0, hid)]
    loss_out[...] = small[:, pl.ds(hid, 1)]
    for copy in copies:
        copy.wait()


def dot(lhs, rhs, dims):
    return lax.dot_general(lhs, rhs, (dims, ((), ())), preferred_element_type=jnp.float32)


def ideal_gain(counts, list_len):
    places = (1 + lax.broadcasted_iota(jnp.int32, (1, list_len), 1)).astype(jnp.float32)
    discount = log_two / jnp.log(1.0 + places)
    total = jnp.zeros((1, 1), jnp.float32)
    start = jnp.zeros((1, 1), jnp.float32)
    for level in reversed(range(len(gain_values))):
        finish = start + counts[level : level + 1, 0:1]
        inside = (places > start) & (places <= finish)
        total = total + gain_values[level] * jnp.sum(jnp.where(inside, discount, 0.0), axis=1, keepdims=True)
        start = finish
    return jnp.maximum(total, 1.0)


def step_kernel(
    chips, spans, lengths, labels, features_hbm, w_first_hbm, b_first, w_second_hbm,
    first_out, second_out, small_out,
    feats, w_first, w_second, feats_t, hidden_t, pre, hidden, emb, keys, slopes, weights, counts, grads, small,
    load_sem, key_s, key_r, weight_s, weight_r, count_s, count_r, *scratch,
):
    dp, span = lax.axis_index("dp"), lax.axis_index("span")
    place = (lax.rem(dp, 2), dp // 2, span)
    rows = feats.shape[0]
    width = w_second.shape[1]
    hid = w_first.shape[1]
    half_width = width // 2
    pair_scale = 1.0 / math.sqrt(half_width)
    pieces = 1 + hid // width
    list_count, list_len = 2 * chips, rows * spans
    loads = [
        pltpu.make_async_copy(src, dst, load_sem.at[n])
        for n, (src, dst) in enumerate(
            ((features_hbm.at[0], feats), (w_first_hbm, w_first), (w_second_hbm, w_second))
        )
    ]
    for load in loads:
        load.start()
    enter = greet_peers(place, chips, spans)

    def to_peers(make_src, dst, send, recv):
        made = []
        for k in range(1, spans):
            copy = pltpu.make_async_remote_copy(
                src_ref=make_src, dst_ref=dst.at[k], send_sem=send.at[k - 1], recv_sem=recv.at[k - 1],
                device_id={"dp": dp, "span": lax.rem(span + k, spans)}, device_id_type=pl.DeviceIdType.MESH,
            )
            copy.start()
            made.append(copy)
        return made

    length = lengths[0]
    slots = lax.broadcasted_iota(jnp.int32, (1, rows), 1)

    def live_row(k):
        owner = lax.rem(span - k + spans, spans)
        return (owner * rows + slots < length).astype(jnp.float32)

    own_live = live_row(0)
    live_col = (span * rows + lax.broadcasted_iota(jnp.int32, (rows, 1), 0) < length).astype(jnp.float32)
    eye = lax.broadcasted_iota(jnp.int32, (rows, rows), 0) == lax.broadcasted_iota(jnp.int32, (rows, rows), 1)
    label_row = labels[...].astype(jnp.float32)
    label_col = jnp.sum(jnp.where(eye, label_row, 0.0), axis=1, keepdims=True)
    gain = jnp.zeros((rows, 1), jnp.float32)
    for level, value in enumerate(gain_values):
        gain = gain + jnp.where(label_col == level, value, 0.0)
    gain = gain * live_col
    levels = lax.broadcasted_iota(jnp.int32, (8, rows), 0).astype(jnp.float32)
    level_counts = jnp.sum(jnp.where(levels == label_row, own_live, 0.0), axis=1, keepdims=True)
    counts[0] = jnp.broadcast_to(level_counts, counts.shape[1:])

    loads[0].wait()
    loads[1].wait()
    for p in range(pieces - 1):
        cols = pl.ds(p * width, width)
        pre_act = dot(feats[...], w_first[:, cols], ((1,), (0,))) + b_first[:, cols]
        pre[:, cols] = pre_act
        hidden[:, cols] = jnp.maximum(pre_act, 0.0).astype(jnp.bfloat16)
    loads[2].wait()
    row_emb = dot(hidden[...], w_second[...], ((1,), (0,))).astype(jnp.bfloat16)
    emb[...] = row_emb
    keys[0] = jnp.concatenate([row_emb[:, half_width:], -row_emb[:, :half_width]], axis=1)
    enter()
    key_copies = to_peers(keys.at[0], keys, key_s, key_r)
    count_copies = to_peers(counts.at[0], counts, count_s, count_r)
    feats_t[...] = feats[...].T
    hidden_t[...] = hidden[...].T

    rank = jnp.full((rows, 1), 0.5, jnp.float32)
    for k in range(spans):
        if k:
            key_copies[k - 1].wait()
        logits = dot(emb[...], keys[k], ((1,), (1,))) * pair_scale
        below = jax.nn.sigmoid(-logits)
        slopes[k] = below * (1.0 - below)
        rank = rank + jnp.sum(below * live_row(k), axis=1, keepdims=True)
    for copy in count_copies:
        copy.wait()
    all_counts = counts[0]
    for k in range(1, spans):
        all_counts = all_counts + counts[k]
    ideal = ideal_gain(all_counts, list_len)
    log_rank = jnp.log(1.0 + rank)
    weight = gain / (ideal * list_count) * log_two / ((1.0 + rank) * log_rank * log_rank)
    weights[0] = jnp.broadcast_to(jnp.sum(jnp.where(eye, weight, 0.0), axis=0, keepdims=True), weights.shape[1:])
    weight_copies = to_peers(weights.at[0], weights, weight_s, weight_r)
    dcg = jnp.sum(gain * log_two / log_rank, axis=0, keepdims=True)
    loss_part = (1.0 / spans - dcg / ideal) / list_count
    small[:, pl.ds(hid, 128)] = jnp.broadcast_to(loss_part, (1, 128))

    total = jnp.zeros((rows, width), jnp.float32)
    for k in range(spans):
        if k:
            weight_copies[k - 1].wait()
        pair_grad = slopes[k] * (live_col * weights[k, 0:1, :] - weight * live_row(k))
        total = total + dot(pair_grad.astype(jnp.bfloat16), keys[k], ((1,), (0,)))
    grad_emb = (total * pair_scale).astype(jnp.bfloat16)

    def result(p, at):
        return second_out.at[at] if p == 0 else first_out.at[at, pl.ds((p - 1) * width, width)]

    red = Reducer(place, chips, spans, grads, result, lambda: small[...], small_out, scratch)
    grads[0] = dot(hidden_t[...], grad_emb, ((1,), (0,)))
    red.pair_out(0)
    for p in range(1, pieces):
        cols = pl.ds((p - 1) * width, width)
        back = dot(grad_emb, w_second[cols, :], ((1,), (1,)))
        grad_pre = jnp.where(pre[:, cols] > 0.0, back, 0.0).astype(jnp.bfloat16)
        small[:, cols] = jnp.sum(grad_pre.astype(jnp.float32), axis=0, keepdims=True)
        grads[p] = dot(feats_t[...], grad_pre, ((1,), (0,)))
        red.pair_out(p)
        red.chip_out(p - 1)
    red.small_first()
    red.chip_out(pieces - 1)
    finish_reduce(red, pieces)


def shards(features, lengths, labels, w_first, b_first, w_second):
    chips, spans = lax.axis_size("dp") // 2, lax.axis_size("span")
    rows, depth = features.shape[1:]
    hid, width = w_second.shape
    pieces = 1 + hid // width
    small_shape = (1, hid + 128)
    vmem, dma = pltpu.VMEM, pltpu.SemaphoreType.DMA
    in_vmem = pl.BlockSpec(memory_space=pltpu.VMEM)
    in_place = pl.BlockSpec(memory_space=pl.ANY)
    first_sum, second_sum, small_sum = pl.pallas_call(
        lambda *refs: step_kernel(chips, spans, *refs),
        name="rank_step",
        out_shape=(
            jax.ShapeDtypeStruct((depth, hid), jnp.bfloat16),
            jax.ShapeDtypeStruct((hid, width), jnp.bfloat16),
            jax.ShapeDtypeStruct(small_shape, jnp.float32),
        ),
        in_specs=[pl.BlockSpec(memory_space=pltpu.SMEM), in_vmem, in_place, in_place, in_vmem, in_place],
        out_specs=(in_vmem,) * 3,
        scratch_shapes=[
            vmem((rows, depth), jnp.bfloat16),
            vmem((depth, hid), jnp.bfloat16),
            vmem((hid, width), jnp.bfloat16),
            vmem((depth, rows), jnp.bfloat16),
            vmem((hid, rows), jnp.bfloat16),
            vmem((rows, hid), jnp.float32),
            vmem((rows, hid), jnp.bfloat16),
            vmem((rows, width), jnp.bfloat16),
            vmem((spans, rows, width), jnp.bfloat16),
            vmem((spans, rows, rows), jnp.float32),
            vmem((spans, 8, rows), jnp.float32),
            vmem((spans, 8, 128), jnp.float32),
            vmem((pieces, hid, width), jnp.float32),
            vmem(small_shape, jnp.float32),
            dma((3,)),
            dma((spans - 1,)), dma((spans - 1,)), dma((spans - 1,)),
            dma((spans - 1,)), dma((spans - 1,)), dma((spans - 1,)),
        ]
        + reducer_scratch(pieces, hid, width, chips, spans, small_shape),
        compiler_params=pltpu.CompilerParams(collective_id=0, has_side_effects=True, vmem_limit_bytes=60 << 20),
    )(lengths, labels, features, w_first, b_first.reshape(1, -1), w_second)
    parts = 4
    first, second, bias, loss = pl.pallas_call(
        write_kernel,
        name="write_out",
        out_shape=(
            jax.ShapeDtypeStruct((depth, hid), jnp.float32),
            jax.ShapeDtypeStruct((hid, width), jnp.float32),
            jax.ShapeDtypeStruct((1, hid), jnp.float32),
            jax.ShapeDtypeStruct((1, 1), jnp.float32),
        ),
        in_specs=[in_vmem] * 3,
        out_specs=(in_place, in_place, in_vmem, in_vmem),
        scratch_shapes=[
            vmem((parts, depth // parts, hid), jnp.float32),
            vmem((hid, width), jnp.float32),
            dma((parts + 1,)),
        ],
    )(first_sum, second_sum, small_sum)
    return loss[0, 0], first, bias[0], second


def solution(mesh):
    placed = (P("dp", "span", None), P("dp"), P("dp", "span"), P(), P(), P())
    return jax.shard_map(
        shards, mesh=mesh, in_specs=placed, out_specs=(P(), P(), P(), P()), check_vma=False
    )
```

```python
import math

import jax
import jax.numpy as jnp
from jax import lax
from jax.experimental import pallas as pl
from jax.experimental.pallas import tpu as pltpu
from jax.sharding import PartitionSpec as P

gain_values = (0.0, 1.0, 3.0, 7.0, 15.0)
log_two = math.log(2.0)


def greet_peers(place, chips, spans):
    core, chip, span = place
    barrier = pltpu.get_barrier_semaphore()
    peers = [{"dp": 2 * chip + 1 - core, "span": span}]
    peers += [{"dp": 2 * lax.rem(chip + k, chips) + core, "span": span} for k in range(1, chips)]
    peers += [{"dp": 2 * chip + core, "span": lax.rem(span + k, spans)} for k in range(1, spans)]
    for peer in peers:
        pl.semaphore_signal(barrier, inc=1, device_id=peer, device_id_type=pl.DeviceIdType.MESH)
    return lambda: pl.semaphore_wait(barrier, len(peers))


def rows_at(start, size):
    return pl.ds(pl.multiple_of(start, size), size)


def owners_of(rows, chips, spans):
    block = rows // 2 // chips
    return min(spans, block // 16)


class Reducer:
    def __init__(self, place, chips, spans, grads, result, small, small_out, scratch):
        self.core, self.chip, self.span = place
        self.chips, self.spans = chips, spans
        self.grads, self.result = grads, result
        self.small, self.small_out = small, small_out
        (
            self.pair_in, self.half_sum, self.half_buf, self.chip_in,
            self.block_sum, self.block_buf, self.span_in,
            self.small_pair, self.small_chip, self.small_span,
            self.pair_s, self.pair_r, self.chip_s, self.chip_r, self.span_s, self.span_r,
            self.small_s, self.small_r,
        ) = scratch
        self.half = self.pair_in.shape[1]
        self.block = self.half // chips
        self.part = self.span_in.shape[2]
        self.owners = self.block // self.part
        self.copies = {}

    def copy(self, key, src, dst, send, recv, dp=None, span=None):
        peer = {
            "dp": 2 * self.chip + self.core if dp is None else dp,
            "span": self.span if span is None else span,
        }
        made = pltpu.make_async_remote_copy(
            src_ref=src, dst_ref=dst, send_sem=send, recv_sem=recv,
            device_id=peer, device_id_type=pl.DeviceIdType.MESH,
        )
        made.start()
        self.copies.setdefault(key, []).append(made)

    def settle(self, key):
        for made in self.copies.pop(key, []):
            made.wait()

    def partner(self):
        return 2 * self.chip + 1 - self.core

    def other_chip(self, k):
        return 2 * lax.rem(self.chip + k, self.chips) + self.core

    def pair_out(self, p):
        away = self.grads.at[p, rows_at((1 - self.core) * self.half, self.half)]
        self.copy(("pair", p), away, self.pair_in.at[p], self.pair_s.at[0, p], self.pair_r.at[0, p], dp=self.partner())

    def chip_out(self, p):
        self.settle(("pair", p))
        own = self.grads[p, rows_at(self.core * self.half, self.half), :]
        total = own + self.pair_in[p]
        self.half_sum[p] = total
        self.half_buf[p] = total.astype(jnp.bfloat16)
        for k in range(1, self.chips):
            rows = rows_at(lax.rem(self.chip + k, self.chips) * self.block, self.block)
            self.copy(("chip", p), self.half_buf.at[p, rows], self.chip_in.at[p, k - 1], self.chip_s.at[0, p, k - 1], self.chip_r.at[0, p, k - 1], dp=self.other_chip(k))

    def span_out(self, p):
        self.settle(("chip", p))
        total = self.half_sum[p, rows_at(self.chip * self.block, self.block)]
        for k in range(1, self.chips):
            total = total + self.chip_in[p, k - 1].astype(jnp.float32)
        self.block_sum[p] = total
        self.block_buf[p] = total.astype(jnp.bfloat16)
        for k in range(1, self.spans):
            to = lax.rem(self.span + k, self.spans)
            rows = rows_at(lax.rem(to, self.owners) * self.part, self.part)
            self.copy(("span", p), self.block_buf.at[p, rows], self.span_in.at[p, k - 1], self.span_s.at[0, p, k - 1], self.span_r.at[0, p, k - 1], span=to)

    def span_back(self, p):
        self.settle(("span", p))
        mine = lax.rem(self.span, self.owners)
        rows = rows_at(mine * self.part, self.part)
        if self.owners == self.spans:
            total = self.block_sum[p, rows]
        else:
            total = self.block_buf[p, rows].astype(jnp.float32)
        for k in range(1, self.spans):
            total = total + self.span_in[p, k - 1].astype(jnp.float32)
        start = self.core * self.half + self.chip * self.block + mine * self.part
        place = self.result(p, rows_at(start, self.part))
        place[...] = total.astype(jnp.bfloat16)
        for k in range(1, self.owners):
            to = self.span - mine + lax.rem(mine + k, self.owners)
            self.copy(("span_back", p), place, place, self.span_s.at[1, p, k - 1], self.span_r.at[1, p, k - 1], span=to)

    def chip_back(self, p):
        self.settle(("span_back", p))
        place = self.result(p, rows_at(self.core * self.half + self.chip * self.block, self.block))
        for k in range(1, self.chips):
            self.copy(("chip_back", p), place, place, self.chip_s.at[1, p, k - 1], self.chip_r.at[1, p, k - 1], dp=self.other_chip(k))

    def pair_back(self, p):
        self.settle(("chip_back", p))
        place = self.result(p, rows_at(self.core * self.half, self.half))
        self.copy(("pair_back", p), place, place, self.pair_s.at[1, p], self.pair_r.at[1, p], dp=self.partner())

    def small_first(self):
        self.small_pair[self.core] = self.small()
        place = self.small_pair.at[self.core]
        self.copy("small0", place, place, self.small_s.at[0], self.small_r.at[0], dp=self.partner())

    def small_second(self):
        self.settle("small0")
        self.small_chip[self.chip] = self.small_pair[0] + self.small_pair[1]
        place = self.small_chip.at[self.chip]
        for k in range(1, self.chips):
            self.copy("small1", place, place, self.small_s.at[k], self.small_r.at[k], dp=self.other_chip(k))

    def small_third(self):
        self.settle("small1")
        total = self.small_chip[0]
        for k in range(1, self.chips):
            total = total + self.small_chip[k]
        self.small_span[self.span] = total
        place = self.small_span.at[self.span]
        for k in range(1, self.spans):
            at = self.chips + k - 1
            self.copy("small2", place, place, self.small_s.at[at], self.small_r.at[at], span=lax.rem(self.span + k, self.spans))

    def small_last(self):
        self.settle("small2")
        total = self.small_span[0]
        for k in range(1, self.spans):
            total = total + self.small_span[k]
        self.small_out[...] = total


def reducer_scratch(pieces, rows, width, chips, spans, small_shape):
    half = rows // 2
    block = half // chips
    part = block // owners_of(rows, chips, spans)
    vmem, dma = pltpu.VMEM, pltpu.SemaphoreType.DMA
    return [
        vmem((pieces, half, width), jnp.float32),
        vmem((pieces, half, width), jnp.float32),
        vmem((pieces, half, width), jnp.bfloat16),
        vmem((pieces, chips - 1, block, width), jnp.bfloat16),
        vmem((pieces, block, width), jnp.float32),
        vmem((pieces, block, width), jnp.bfloat16),
        vmem((pieces, spans - 1, part, width), jnp.bfloat16),
        vmem((2,) + small_shape, jnp.float32),
        vmem((chips,) + small_shape, jnp.float32),
        vmem((spans,) + small_shape, jnp.float32),
        dma((2, pieces)), dma((2, pieces)),
        dma((2, pieces, chips - 1)), dma((2, pieces, chips - 1)),
        dma((2, pieces, spans - 1)), dma((2, pieces, spans - 1)),
        dma((chips + spans,)), dma((chips + spans,)),
    ]


def finish_reduce(red, pieces):
    stages = (red.span_out, red.span_back, red.chip_back, red.pair_back, lambda p: red.settle(("pair_back", p)))
    order = sorted((p + lag, n, p) for p in range(pieces) for n, lag in enumerate((0, 2.2, 4.3, 6.5, 9.0)))
    smalls = {0: red.small_second, 3: red.small_third, 8: red.small_last}
    for at, (_, n, p) in enumerate(order):
        stages[n](p)
        if at in smalls:
            smalls[at]()


def write_kernel(first, second, small, first_out, second_out, bias_out, loss_out, first_buf, second_buf, sem):
    parts = first_buf.shape[0]
    rows = first_buf.shape[1]
    copies = [pltpu.make_async_copy(second_buf, second_out, sem.at[parts])]
    second_buf[...] = second[...].astype(jnp.float32)
    copies[0].start()
    for n in range(parts):
        at = pl.ds(n * rows, rows)
        first_buf[n] = first[at, :].astype(jnp.float32)
        copies.append(pltpu.make_async_copy(first_buf.at[n], first_out.at[at], sem.at[n]))
        copies[-1].start()
    hid = bias_out.shape[1]
    bias_out[...] = small[:, pl.ds(0, hid)]
    loss_out[...] = small[:, pl.ds(hid, 1)]
    for copy in copies:
        copy.wait()


def dot(lhs, rhs, dims):
    return lax.dot_general(lhs, rhs, (dims, ((), ())), preferred_element_type=jnp.float32)


def ideal_gain(counts, list_len):
    places = (1 + lax.broadcasted_iota(jnp.int32, (1, list_len), 1)).astype(jnp.float32)
    discount = log_two / jnp.log(1.0 + places)
    total = jnp.zeros((1, 1), jnp.float32)
    start = jnp.zeros((1, 1), jnp.float32)
    for level in reversed(range(len(gain_values))):
        finish = start + counts[level : level + 1, 0:1]
        inside = (places > start) & (places <= finish)
        total = total + gain_values[level] * jnp.sum(jnp.where(inside, discount, 0.0), axis=1, keepdims=True)
        start = finish
    return jnp.maximum(total, 1.0)


def step_kernel(
    chips, spans, lengths, labels, features_hbm, w_first_hbm, b_first, w_second_hbm,
    first_out, second_out, small_out,
    feats, w_first, w_second, feats_t, hidden_t, pre, hidden, emb, keys, slopes, weights, counts, grads, small,
    load_sem, key_s, key_r, weight_s, weight_r, count_s, count_r, *scratch,
):
    dp, span = lax.axis_index("dp"), lax.axis_index("span")
    place = (lax.rem(dp, 2), dp // 2, span)
    rows = feats.shape[0]
    width = w_second.shape[1]
    hid = w_first.shape[1]
    half_width = width // 2
    pair_scale = 1.0 / math.sqrt(half_width)
    pieces = 1 + hid // width
    list_count, list_len = 2 * chips, rows * spans
    loads = [
        pltpu.make_async_copy(src, dst, load_sem.at[n])
        for n, (src, dst) in enumerate(
            ((features_hbm.at[0], feats), (w_first_hbm, w_first), (w_second_hbm, w_second))
        )
    ]
    for load in loads:
        load.start()
    enter = greet_peers(place, chips, spans)

    def to_peers(make_src, dst, send, recv):
        made = []
        for k in range(1, spans):
            copy = pltpu.make_async_remote_copy(
                src_ref=make_src, dst_ref=dst.at[k], send_sem=send.at[k - 1], recv_sem=recv.at[k - 1],
                device_id={"dp": dp, "span": lax.rem(span + k, spans)}, device_id_type=pl.DeviceIdType.MESH,
            )
            copy.start()
            made.append(copy)
        return made

    length = lengths[0]
    slots = lax.broadcasted_iota(jnp.int32, (1, rows), 1)

    def live_row(k):
        owner = lax.rem(span - k + spans, spans)
        return (owner * rows + slots < length).astype(jnp.float32)

    own_live = live_row(0)
    live_col = (span * rows + lax.broadcasted_iota(jnp.int32, (rows, 1), 0) < length).astype(jnp.float32)
    eye = lax.broadcasted_iota(jnp.int32, (rows, rows), 0) == lax.broadcasted_iota(jnp.int32, (rows, rows), 1)
    label_row = labels[...].astype(jnp.float32)
    label_col = jnp.sum(jnp.where(eye, label_row, 0.0), axis=1, keepdims=True)
    gain = jnp.zeros((rows, 1), jnp.float32)
    for level, value in enumerate(gain_values):
        gain = gain + jnp.where(label_col == level, value, 0.0)
    gain = gain * live_col
    levels = lax.broadcasted_iota(jnp.int32, (8, rows), 0).astype(jnp.float32)
    level_counts = jnp.sum(jnp.where(levels == label_row, own_live, 0.0), axis=1, keepdims=True)
    counts[0] = jnp.broadcast_to(level_counts, counts.shape[1:])

    loads[0].wait()
    loads[1].wait()
    for p in range(pieces - 1):
        cols = pl.ds(p * width, width)
        pre_act = dot(feats[...], w_first[:, cols], ((1,), (0,))) + b_first[:, cols]
        pre[:, cols] = pre_act
        hidden[:, cols] = jnp.maximum(pre_act, 0.0).astype(jnp.bfloat16)
    loads[2].wait()
    row_emb = dot(hidden[...], w_second[...], ((1,), (0,))).astype(jnp.bfloat16)
    emb[...] = row_emb
    keys[0] = jnp.concatenate([row_emb[:, half_width:], -row_emb[:, :half_width]], axis=1)
    enter()
    key_copies = to_peers(keys.at[0], keys, key_s, key_r)
    count_copies = to_peers(counts.at[0], counts, count_s, count_r)
    feats_t[...] = feats[...].T
    hidden_t[...] = hidden[...].T

    rank = jnp.full((rows, 1), 0.5, jnp.float32)
    for k in range(spans):
        if k:
            key_copies[k - 1].wait()
        logits = dot(emb[...], keys[k], ((1,), (1,))) * pair_scale
        below = jax.nn.sigmoid(-logits)
        slopes[k] = below * (1.0 - below)
        rank = rank + jnp.sum(below * live_row(k), axis=1, keepdims=True)
    for copy in count_copies:
        copy.wait()
    all_counts = counts[0]
    for k in range(1, spans):
        all_counts = all_counts + counts[k]
    ideal = ideal_gain(all_counts, list_len)
    log_rank = jnp.log(1.0 + rank)
    weight = gain / (ideal * list_count) * log_two / ((1.0 + rank) * log_rank * log_rank)
    weights[0] = jnp.broadcast_to(jnp.sum(jnp.where(eye, weight, 0.0), axis=0, keepdims=True), weights.shape[1:])
    weight_copies = to_peers(weights.at[0], weights, weight_s, weight_r)
    dcg = jnp.sum(gain * log_two / log_rank, axis=0, keepdims=True)
    loss_part = (1.0 / spans - dcg / ideal) / list_count
    small[:, pl.ds(hid, 128)] = jnp.broadcast_to(loss_part, (1, 128))

    total = jnp.zeros((rows, width), jnp.float32)
    for k in range(spans):
        if k:
            weight_copies[k - 1].wait()
        pair_grad = slopes[k] * (live_col * weights[k, 0:1, :] - weight * live_row(k))
        total = total + dot(pair_grad.astype(jnp.bfloat16), keys[k], ((1,), (0,)))
    grad_emb = (total * pair_scale).astype(jnp.bfloat16)

    def result(p, at):
        return second_out.at[at] if p == 0 else first_out.at[at, pl.ds((p - 1) * width, width)]

    red = Reducer(place, chips, spans, grads, result, lambda: small[...], small_out, scratch)
    grads[0] = dot(hidden_t[...], grad_emb, ((1,), (0,)))
    red.pair_out(0)
    for p in range(1, pieces):
        cols = pl.ds((p - 1) * width, width)
        back = dot(grad_emb, w_second[cols, :], ((1,), (1,)))
        grad_pre = jnp.where(pre[:, cols] > 0.0, back, 0.0).astype(jnp.bfloat16)
        small[:, cols] = jnp.sum(grad_pre.astype(jnp.float32), axis=0, keepdims=True)
        grads[p] = dot(feats_t[...], grad_pre, ((1,), (0,)))
        red.pair_out(p)
        if p > 1:
            red.chip_out(p - 2)
    red.small_first()
    for p in range(max(pieces - 2, 0), pieces):
        red.chip_out(p)
    finish_reduce(red, pieces)


def shards(features, lengths, labels, w_first, b_first, w_second):
    chips, spans = lax.axis_size("dp") // 2, lax.axis_size("span")
    rows, depth = features.shape[1:]
    hid, width = w_second.shape
    pieces = 1 + hid // width
    small_shape = (1, hid + 128)
    vmem, dma = pltpu.VMEM, pltpu.SemaphoreType.DMA
    in_vmem = pl.BlockSpec(memory_space=pltpu.VMEM)
    in_place = pl.BlockSpec(memory_space=pl.ANY)
    first_sum, second_sum, small_sum = pl.pallas_call(
        lambda *refs: step_kernel(chips, spans, *refs),
        name="rank_step",
        out_shape=(
            jax.ShapeDtypeStruct((depth, hid), jnp.bfloat16),
            jax.ShapeDtypeStruct((hid, width), jnp.bfloat16),
            jax.ShapeDtypeStruct(small_shape, jnp.float32),
        ),
        in_specs=[pl.BlockSpec(memory_space=pltpu.SMEM), in_vmem, in_place, in_place, in_vmem, in_place],
        out_specs=(in_vmem,) * 3,
        scratch_shapes=[
            vmem((rows, depth), jnp.bfloat16),
            vmem((depth, hid), jnp.bfloat16),
            vmem((hid, width), jnp.bfloat16),
            vmem((depth, rows), jnp.bfloat16),
            vmem((hid, rows), jnp.bfloat16),
            vmem((rows, hid), jnp.float32),
            vmem((rows, hid), jnp.bfloat16),
            vmem((rows, width), jnp.bfloat16),
            vmem((spans, rows, width), jnp.bfloat16),
            vmem((spans, rows, rows), jnp.float32),
            vmem((spans, 8, rows), jnp.float32),
            vmem((spans, 8, 128), jnp.float32),
            vmem((pieces, hid, width), jnp.float32),
            vmem(small_shape, jnp.float32),
            dma((3,)),
            dma((spans - 1,)), dma((spans - 1,)), dma((spans - 1,)),
            dma((spans - 1,)), dma((spans - 1,)), dma((spans - 1,)),
        ]
        + reducer_scratch(pieces, hid, width, chips, spans, small_shape),
        compiler_params=pltpu.CompilerParams(collective_id=0, has_side_effects=True, vmem_limit_bytes=60 << 20),
    )(lengths, labels, features, w_first, b_first.reshape(1, -1), w_second)
    parts = 4
    first, second, bias, loss = pl.pallas_call(
        write_kernel,
        name="write_out",
        out_shape=(
            jax.ShapeDtypeStruct((depth, hid), jnp.float32),
            jax.ShapeDtypeStruct((hid, width), jnp.float32),
            jax.ShapeDtypeStruct((1, hid), jnp.float32),
            jax.ShapeDtypeStruct((1, 1), jnp.float32),
        ),
        in_specs=[in_vmem] * 3,
        out_specs=(in_place, in_place, in_vmem, in_vmem),
        scratch_shapes=[
            vmem((parts, depth // parts, hid), jnp.float32),
            vmem((hid, width), jnp.float32),
            dma((parts + 1,)),
        ],
    )(first_sum, second_sum, small_sum)
    return loss[0, 0], first, bias[0], second


def solution(mesh):
    placed = (P("dp", "span", None), P("dp"), P("dp", "span"), P(), P(), P())
    return jax.shard_map(
        shards, mesh=mesh, in_specs=placed, out_specs=(P(), P(), P(), P()), check_vma=False
    )
```
